256 devices in a mesh: dp: 4 (over x), vocab: 64 (over y, z, core).
Axes of the slice: x: 4, y: 4, z: 8, core: 2. Of those that a mesh axis runs over, the one named last changes fastest.
Arguments:
- hidden: bfloat16 [1024, 4096], P(('dp', 'vocab')), may hold values from -48 to 48
- weight: bfloat16 [65536, 4096], P('vocab'), may hold values from -3 to 3
- teacher: bfloat16 [1024, 8192], P('dp', 'vocab'), may hold values from 0 to 0.002, as said below
- block_ids: int32 [8, 64], P('dp'), may hold values from 0 to 511, as said below
Outputs:
- grad_hidden: bfloat16 [1024, 4096], P(('dp', 'vocab'))
- grad_weight: bfloat16 [65536, 4096], P('vocab', 'dp')
The draws below stay inside these ranges and needn't reach their ends.
Inputs may be any that keep to these rules, and one draw needn't show every extreme that they name: `block_ids`: row b lists 64 different vocabulary blocks in no fixed order; frequent blocks recur over many rows. `teacher`: all entries are positive.
All inputs are finite; a program needn't handle non-finite values.
Results may differ from the reference program's by a relative error of at most 0.0051.
Values may be sent and summed in bfloat16 or wider, within the bound.
A program may use at most 128 MiB of HBM per device.

```python
import math
import jax
import jax.numpy as jnp
from jax import lax

D = 4096
BLK = 128
K = 64
VB = 512
TOKENS = 1024
TB = 8


def weight_row(key, vocab_index):
    noise_row = jnp.clip(jax.random.normal(jax.random.fold_in(jax.random.fold_in(key, 31), vocab_index), (D,), jnp.float32), -6.0, 6.0)
    row_level = jnp.exp(jax.random.uniform(jax.random.fold_in(jax.random.fold_in(key, 32), vocab_index), (), jnp.float32, math.log(0.3), 0.0))
    row_level = row_level * (1.0 + 2.0 * vocab_index.astype(jnp.float32) / (VB * BLK))
    row_value = noise_row * row_level / math.sqrt(D)
    return row_value.astype(jnp.bfloat16).astype(jnp.float32)


def draw_weight(key, part):
    indices = jnp.arange(VB * BLK, dtype=jnp.int32)
    rows = jax.vmap(lambda index: weight_row(key, index))(indices)
    return rows.astype(jnp.bfloat16)


def draw_hidden(key, part):
    values = jnp.clip(jax.random.normal(jax.random.fold_in(key, 21), (TOKENS, D), jnp.float32), -6.0, 6.0)
    return values.astype(jnp.bfloat16)


def draw_teacher(key, part):
    slot_of = (jnp.arange(K * BLK, dtype=jnp.int32) // BLK).astype(jnp.float32)
    factor = 0.5 + slot_of / (K - 1)
    values = jnp.exp(jax.random.uniform(jax.random.fold_in(key, 41), (TOKENS, K * BLK), jnp.float32, math.log(1e-06), math.log(0.0008)))
    return (values * factor[None, :]).astype(jnp.bfloat16)


def draw_block_ids(key, part):
    popularity = jax.random.randint(jax.random.fold_in(key, 51), (VB,), 0, 4, jnp.int32)
    noise = jax.random.randint(jax.random.fold_in(key, 52), (TB, VB), 0, 1024, jnp.int32)
    block_range = jnp.arange(VB, dtype=jnp.int32)
    row_range = jnp.arange(TB, dtype=jnp.int32)
    forced = (row_range[:, None] == 0) & (block_range[None, :] == 0) | (row_range[:, None] == TB - 1) & (block_range[None, :] == VB - 1)
    scores = noise + 256 * popularity[None, :] + 4096 * forced.astype(jnp.int32)
    scores = scores * VB + block_range[None, :]
    top_scores, chosen = lax.top_k(scores, K)
    order_keys = jax.random.randint(jax.random.fold_in(key, 53), (TB, K), 0, 65536, jnp.int32) * K + jnp.arange(K, dtype=jnp.int32)[None, :]
    order = jnp.argsort(order_keys, axis=1, stable=True)
    return jnp.take_along_axis(chosen.astype(jnp.int32), order.astype(jnp.int32), axis=1).astype(jnp.int32)


def setup_inputs(seed: int = 0) -> dict:
    arg_keys = jax.random.split(jax.random.key(seed), 5)
    hidden = draw_hidden(jax.random.fold_in(arg_keys[4], 71), 0)
    weight = draw_weight(jax.random.fold_in(arg_keys[4], 71), 0)
    teacher = draw_teacher(jax.random.fold_in(arg_keys[4], 71), 0)
    block_ids = draw_block_ids(jax.random.fold_in(arg_keys[4], 71), 0)
    return dict(hidden=hidden, weight=weight, teacher=teacher, block_ids=block_ids)


loss_scale = 1024.0


def reference(hidden, weight, teacher, block_ids):
    logits = jnp.dot(hidden, weight.T, preferred_element_type=jnp.float32)
    row_top = jnp.max(logits, axis=1, keepdims=True)
    exp_terms = jnp.exp(logits - row_top)
    row_total = jnp.sum(exp_terms, axis=1, keepdims=True)
    teacher_tiles = teacher.astype(jnp.float32).reshape(TB, BLK, K, BLK)
    row_mass = jnp.sum(teacher_tiles, axis=(2, 3)).reshape(TOKENS, 1)
    placed = jnp.zeros((TB, VB, BLK, BLK), jnp.float32)
    rows_index = jnp.arange(TB, dtype=jnp.int32)[:, None]
    placed = placed.at[rows_index, block_ids.astype(jnp.int32)].set(jnp.transpose(teacher_tiles, (0, 2, 1, 3)))
    target = jnp.transpose(placed, (0, 2, 1, 3)).reshape(TOKENS, VB * BLK)
    grad_logits = (loss_scale * (row_mass * (exp_terms / row_total) - target)).astype(jnp.bfloat16)
    grad_hidden = jnp.dot(grad_logits, weight, preferred_element_type=jnp.float32).astype(jnp.bfloat16)
    grad_weight = jnp.dot(grad_logits.T, hidden, preferred_element_type=jnp.float32).astype(jnp.bfloat16)
    return (grad_hidden, grad_weight)
```

```python
import jax
import jax.numpy as jnp
from jax import lax
from jax.experimental import pallas as pl
from jax.experimental.pallas import tpu as pltpu
from jax.sharding import PartitionSpec as P

BLK = 128
loss_scale = 1024.0
BF = jnp.bfloat16
F32 = jnp.float32
MESH = pl.DeviceIdType.MESH

D = 4096
V = 1024
T = 256
DC = 1024
NX, NY, NZ = 4, 4, 8


def ring(buf, n, pos, device, unit, half, ssem, rsem):
    h = n // 2

    def copy(way, step):
        sign = 1 if way == 0 else -1
        origin = lax.rem(pos - sign * (step - 1) + n, n)
        ref = unit(origin) if step < h else half(origin, way)
        return pltpu.make_async_remote_copy(
            src_ref=ref, dst_ref=ref, send_sem=ssem.at[way, step - 1],
            recv_sem=rsem.at[way, step - 1],
            device_id=device(lax.rem(pos + sign + n, n)), device_id_type=MESH)

    def arrival(way, step):
        sign = 1 if way == 0 else -1
        origin = lax.rem(pos - sign * step + n, n)
        ref = unit(origin) if step < h else half(origin, way)
        return pltpu.make_async_remote_copy(
            src_ref=ref, dst_ref=ref, send_sem=ssem.at[way, step - 1],
            recv_sem=rsem.at[way, step - 1],
            device_id=device(lax.rem(pos + sign + n, n)), device_id_type=MESH)

    def start(step):
        for way in range(2):
            copy(way, step).start()

    def arrive(step):
        for way in range(2):
            arrival(way, step).wait_recv()

    def drain():
        for step in range(1, h + 1):
            for way in range(2):
                copy(way, step).wait_send()

    return start, arrive, drain, h


def kernel(hidden_ref, weight_ref, teacher_ref, sel_ref, gh_ref, gw_ref,
           w, hraw, hid, tea, craw, hidc, rel, logits, gt, g, graw, pair, ssum, r1, s2, s2f, r2,
           st0, st1, st2s, st2, acc,
           loc_sem, hs, hr, hfs, hfr, ts, tr, tfs, tfr, xs, xr, xfs, xfr,
           s1s, s1r, s2s, s2r, gs, gr, ps, pr, r1s, r1r, r2s, r2r):
    d = lax.axis_index("dp")
    v = lax.axis_index("vocab")
    y = v // (2 * NZ)
    z = lax.rem(v // 2, NZ)
    c = lax.rem(v, 2)
    me = lax.rem(v, 2 * NZ)

    def dev(yy, zz, cc):
        return {"dp": d, "vocab": (yy * NZ + zz) * 2 + cc}

    def xdev(dd):
        return {"dp": dd, "vocab": v}

    sib = dev(y, z, 1 - c)
    dr, dl, do = lax.rem(d + 1, NX), lax.rem(d + 3, NX), lax.rem(d + 2, NX)

    def remote(src, dst, s, r, device):
        return pltpu.make_async_remote_copy(src_ref=src, dst_ref=dst, send_sem=s, recv_sem=r,
                                            device_id=device, device_id_type=MESH)

    copy_h = pltpu.make_async_copy(hidden_ref, hraw.at[y, z, c], loc_sem.at[0])
    copy_t = pltpu.make_async_copy(teacher_ref, tea.at[y, z, c], loc_sem.at[1])
    copy_w = pltpu.make_async_copy(weight_ref, w, loc_sem.at[2])
    copy_h.start()
    copy_t.start()
    copy_w.start()

    barrier = pltpu.get_barrier_semaphore()
    for k in range(1, 16):
        p = lax.rem(me + k, 16)
        pl.semaphore_signal(barrier, inc=1, device_id=dev(y, p // 2, lax.rem(p, 2)),
                            device_id_type=MESH)
    for k in range(1, NY):
        pl.semaphore_signal(barrier, inc=1, device_id=dev(lax.rem(y + k, NY), z, c),
                            device_id_type=MESH)
    for dd in (dr, dl):
        pl.semaphore_signal(barrier, inc=1, device_id=xdev(dd), device_id_type=MESH)
    pl.semaphore_wait(barrier, 20)

    def gather(buf, half_of, ssem, rsem, fss, frs):
        def build(cc):
            def y_first(o):
                return buf.at[o, z, cc]

            def z_first(o):
                return buf.at[y, o, cc]

            if cc == 0:
                one = ring(buf, NY, y, lambda o: dev(o, z, cc), y_first,
                           lambda o, way: half_of(buf.at[o, z, cc], way),
                           ssem.at[0], rsem.at[0])
                unit = lambda o: buf.at[:, o, cc]
                two = ring(buf, NZ, z, lambda o: dev(y, o, cc), unit,
                           lambda o, way: buf.at[pl.ds(2 * way, 2), o, cc],
                           ssem.at[1], rsem.at[1])
                pos, n = z, NZ
            else:
                one = ring(buf, NZ, z, lambda o: dev(y, o, cc), z_first,
                           lambda o, way: half_of(buf.at[y, o, cc], way),
                           ssem.at[0], rsem.at[0])
                unit = lambda o: buf.at[o, :, cc]
                two = ring(buf, NY, y, lambda o: dev(o, z, cc), unit,
                           lambda o, way: buf.at[o, pl.ds(4 * way, 4), cc],
                           ssem.at[1], rsem.at[1])
                pos, n = y, NY

            def forward(k):
                o = lax.rem(pos + k, n)
                return remote(unit(o), unit(o), fss.at[k], frs.at[k], sib)

            steps = []
            h1, h2 = one[3], two[3]

            def first():
                one[0](1)

            steps.append(first)
            for s in range(2, h1 + 1):
                def mid(s=s):
                    one[1](s - 1)
                    one[0](s)
                steps.append(mid)

            def join():
                one[1](h1)
                two[0](1)
                forward(0).start()

            steps.append(join)
            for s in range(2, h2 + 1):
                def mid2(s=s):
                    two[1](s - 1)
                    two[0](s)
                    forward(s - 1).start()
                    forward(n - s + 1).start()
                steps.append(mid2)

            def last():
                two[1](h2)
                forward(h2).start()

            steps.append(last)

            def drain():
                one[2]()
                two[2]()
                for k in range(n):
                    forward(k).wait_send()

            def from_sibling():
                for k in range(n):
                    o = lax.rem(pos + k, n)
                    remote(unit(o), unit(o), fss.at[k], frs.at[k], sib).wait_recv()

            return steps, drain, from_sibling

        a, b = build(0), build(1)

        def both(fa, fb):
            def run():
                pl.when(c == 0)(fa)
                pl.when(c == 1)(fb)
            return run

        steps = [both(fa, fb) for fa, fb in zip(a[0], b[0])]
        return steps, both(a[1], b[1]), both(b[2], a[2])

    h_steps, h_drain, h_sib = gather(
        hraw, lambda ref, way: ref.at[:, pl.ds(way * (D // 2), D // 2)], hs, hr, hfs, hfr)
    t_steps, t_drain, t_sib = gather(tea, lambda ref, way: ref.at[way], ts, tr, tfs, tfr)

    copy_h.wait()
    for step in h_steps[:-1]:
        step()
    copy_t.wait()
    t_steps[0]()
    h_steps[-1]()

    def cols(dd):
        return pl.ds(pl.multiple_of(dd * DC, DC), DC)

    x_sends = [
        remote(hraw.at[0:2, :, c, :, cols(do)], rel.at[0], xs.at[0], xr.at[0], xdev(dr)),
        remote(hraw.at[2:4, :, c, :, cols(do)], rel.at[1], xs.at[1], xr.at[1], xdev(dl)),
        remote(hraw.at[:, :, c, :, cols(dr)], craw.at[d, :, :, c], xs.at[2], xr.at[2], xdev(dr)),
        remote(hraw.at[:, :, c, :, cols(dl)], craw.at[d, :, :, c], xs.at[3], xr.at[3], xdev(dl)),
    ]
    for copy in x_sends:
        copy.start()
    x_relays = [
        remote(rel.at[0], craw.at[dl, 0:2, :, c], xs.at[4], xr.at[4], xdev(dr)),
        remote(rel.at[1], craw.at[dr, 2:4, :, c], xs.at[5], xr.at[5], xdev(dl)),
    ]

    t_steps[1]()
    h_sib()

    def flatten(i, _):
        yy, zz = i // 4, lax.rem(i, 4)
        hid[pl.ds(pl.multiple_of(16 * i, 16), 16), :] = hraw[yy, pl.ds(2 * zz, 2)].reshape(16, D)
        return 0

    lax.fori_loop(0, 16, flatten, 0)
    t_steps[2]()

    copy_w.wait()
    top = jnp.full((1, T), -jnp.inf, F32)
    for q in range(4):
        rows = pl.ds(256 * q, 256)
        part = lax.dot_general(w[rows, :], hid[...], (((1,), (1,)), ((), ())),
                               preferred_element_type=F32)
        logits[rows, :] = part
        top = jnp.maximum(top, jnp.max(part, axis=0, keepdims=True))
        if q == 1:
            t_steps[3]()
    total = jnp.zeros((1, T), F32)
    for q in range(4):
        rows = pl.ds(256 * q, 256)
        total = total + jnp.sum(jnp.exp(logits[rows, :] - top), axis=0, keepdims=True)
    mass = lax.dot_general(jnp.ones((8, BLK), BF), tea[y, z, c].reshape(T, BLK),
                           (((1,), (1,)), ((), ())), preferred_element_type=F32)[0:1]
    st0[0:1, :] = top
    st0[1:2, :] = total
    st0[2:3, :] = mass
    st0[3:4, :] = mass
    for k in range(1, 16):
        p = lax.rem(me + k, 16)
        remote(st0, st1.at[me], s1s.at[k], s1r.at[me], dev(y, p // 2, lax.rem(p, 2))).start()
    t_steps[4]()
    for k in range(1, 16):
        p = lax.rem(me + k, 16)
        remote(st0, st1.at[p], s1s.at[k], s1r.at[p], dev(y, p // 2, lax.rem(p, 2))).wait_recv()

    def merge(parts):
        m = parts[0][0:1]
        for part in parts[1:]:
            m = jnp.maximum(m, part[0:1])
        s = jnp.zeros((1, T), F32)
        a = jnp.zeros((1, T), F32)
        for part in parts:
            s = s + part[1:2] * jnp.exp(part[0:1] - m)
            a = a + part[2:3]
        return m, s, a

    m1, s1, a1 = merge([st0[...]] + [st1[lax.rem(me + k, 16)] for k in range(1, 16)])
    st2s[0:1, :] = m1
    st2s[1:2, :] = s1
    st2s[2:3, :] = a1
    st2s[3:4, :] = a1
    for k in range(1, NY):
        p = lax.rem(y + k, NY)
        remote(st2s, st2.at[y], s2s.at[k], s2r.at[y], dev(p, z, c)).start()
    t_steps[5]()
    for k in range(1, NY):
        p = lax.rem(y + k, NY)
        remote(st2s, st2.at[p], s2s.at[k], s2r.at[p], dev(p, z, c)).wait_recv()
    m2, s2_, a2 = merge([st2s[...]] + [st2[lax.rem(y + k, NY)] for k in range(1, NY)])
    scale = loss_scale * a2 / s2_

    x_sends[0].wait_recv()
    x_relays[0].start()
    x_sends[1].wait_recv()
    x_relays[1].start()
    t_steps[6]()
    t_sib()

    def grads(j, _):
        rows = pl.ds(pl.multiple_of(j * BLK, BLK), BLK)
        for tb in range(2):
            k = sel_ref[tb * 8 + j]
            found = jnp.where(k >= 0, loss_scale, 0.0)
            kk = jnp.maximum(k, 0)
            tile = tea[kk // 16, lax.rem(kk // 2, NZ), lax.rem(kk, 2), tb]
            part = slice(tb * BLK, tb * BLK + BLK)
            value = (scale[:, part] * jnp.exp(logits[rows, part] - m2[:, part])
                     - found * tile.astype(F32).T)
            gt[d, rows, part] = value.astype(BF)
        return 0

    lax.fori_loop(0, 8, grads, 0)

    def chunk(dd, q):
        return gt.at[dd, pl.ds(256 * q, 256)]

    g_own = []
    for i in range(4):
        for way, q, to in ((0, i, dr), (1, (i + 2) % 4, dl)):
            copy = remote(chunk(d, q), chunk(d, q), gs.at[way, i], gr.at[way, i], xdev(to))
            copy.start()
            g_own.append(copy)

    def g_arrived(way, i):
        q, origin = ((i, dl), ((i + 2) % 4, dr))[way]
        to = (dr, dl)[way]
        remote(chunk(origin, q), chunk(origin, q), gs.at[way, i], gr.at[way, i],
               xdev(to)).wait_recv()

    def g_relay(way, i):
        q, origin = ((i, dl), ((i + 2) % 4, dr))[way]
        to = (dr, dl)[way]
        return remote(chunk(origin, q), chunk(origin, q), gs.at[way, 4 + i], gr.at[way, 4 + i],
                      xdev(to))

    g[...] = gt[d].T

    def back(i, _):
        span = pl.ds(pl.multiple_of(i * 512, 512), 512)
        part = jnp.dot(g[...], w[:, span], preferred_element_type=F32)
        graw[:, :, :, :, span] = part.reshape(NY, NZ, 2, 4, 512).astype(BF)
        return 0

    lax.fori_loop(0, 8, back, 0)

    swap = remote(graw.at[:, :, 1 - c], pair, ps.at[0], pr.at[0], sib)
    swap.start()
    for i in range(2):
        for way in range(2):
            g_arrived(way, i)
            g_relay(way, i).start()
    swap.wait_recv()

    def add_pair(i, _):
        yy, zz = i // NZ, lax.rem(i, NZ)
        ssum[yy, zz] = (graw[yy, zz, c].astype(F32) + pair[yy, zz].astype(F32)).astype(BF)
        return 0

    lax.fori_loop(0, 32, add_pair, 0)

    def reduce_steps(cc):
        if cc == 0:
            n1, p1, n2, p2 = NZ, z, NY, y
            piece = lambda o: ssum.at[:, o]
            own = lambda o: graw[o, z, cc].astype(F32) + pair[o, z].astype(F32)
            dev1, dev2 = (lambda o: dev(y, o, cc)), (lambda o: dev(o, z, cc))
        else:
            n1, p1, n2, p2 = NY, y, NZ, z
            piece = lambda o: ssum.at[o]
            own = lambda o: graw[y, o, cc].astype(F32) + pair[y, o].astype(F32)
            dev1, dev2 = (lambda o: dev(o, z, cc)), (lambda o: dev(y, o, cc))

        def slot(o):
            return r1.at[pl.ds(o * n2, n2)]

        def one(k):
            o = lax.rem(p1 + k, n1)
            return remote(piece(o), slot(p1), r1s.at[k], r1r.at[p1], dev1(o))

        def one_in(k):
            o = lax.rem(p1 + k, n1)
            return remote(piece(o), slot(o), r1s.at[k], r1r.at[o], dev1(o))

        def two(k):
            o = lax.rem(p2 + k, n2)
            return remote(s2.at[o], r2.at[p2], r2s.at[k], r2r.at[p2], dev2(o))

        def two_in(k):
            o = lax.rem(p2 + k, n2)
            return remote(s2.at[o], r2.at[o], r2s.at[k], r2r.at[o], dev2(o))

        def start():
            for k in range(1, n1):
                one(k).start()

        def middle():
            for k in range(1, n1):
                one_in(k).wait_recv()

            def add(i, _):
                total = own(i)
                for k in range(1, n1):
                    total = total + r1[lax.rem(p1 + k, n1) * n2 + i].astype(F32)
                s2f[i] = total
                s2[i] = total.astype(BF)
                return 0

            lax.fori_loop(0, n2, add, 0)
            for k in range(1, n2):
                two(k).start()

        def finish():
            for k in range(1, n2):
                two_in(k).wait_recv()
            total = s2f[p2]
            for k in range(1, n2):
                total = total + r2[lax.rem(p2 + k, n2)].astype(F32)
            gh_ref[...] = total.astype(BF)
            for k in range(1, n1):
                one(k).wait_send()
            for k in range(1, n2):
                two(k).wait_send()

        return start, middle, finish

    ra, rb = reduce_steps(0), reduce_steps(1)

    def phase(i):
        pl.when(c == 0)(ra[i])
        pl.when(c == 1)(rb[i])

    phase(0)

    x_sends[2].wait_recv()
    x_sends[3].wait_recv()
    x_relays[0].wait_recv()
    x_relays[1].wait_recv()
    x_fwd = [remote(craw.at[dd, :, :, c], craw.at[dd, :, :, c], xfs.at[i], xfr.at[i], sib)
             for i, dd in enumerate((dl, dr, do))]
    for copy in x_fwd:
        copy.start()
    for i, dd in enumerate((dl, dr, do)):
        remote(craw.at[dd, :, :, 1 - c], craw.at[dd, :, :, 1 - c], xfs.at[i], xfr.at[i],
               sib).wait_recv()
    for dd in (dl, dr, do):
        def flatten_cols(i, _, dd=dd):
            yy, zz = i // 4, lax.rem(i, 4)
            hidc[dd, pl.ds(pl.multiple_of(16 * i, 16), 16), :] = (
                craw[dd, yy, pl.ds(2 * zz, 2)].reshape(16, DC))
            return 0

        lax.fori_loop(0, 16, flatten_cols, 0)
    hidc[d] = hid[:, cols(d)]

    for i in range(2, 4):
        for way in range(2):
            g_arrived(way, i)

    def near(q, _):
        rows = pl.ds(pl.multiple_of(q * 256, 256), 256)
        part = jnp.dot(gt[d, rows], hidc[d], preferred_element_type=F32)
        part = part + jnp.dot(gt[dl, rows], hidc[dl], preferred_element_type=F32)
        part = part + jnp.dot(gt[dr, rows], hidc[dr], preferred_element_type=F32)
        acc[rows, :] = part
        return 0

    lax.fori_loop(0, 4, near, 0)
    phase(1)

    for i in range(2):
        for way, q in ((0, i), (1, (i + 2) % 4)):
            remote(chunk(do, q), chunk(do, q), gs.at[way, 4 + i], gr.at[way, 4 + i],
                   xdev((dr, dl)[way])).wait_recv()

    def far(q, _):
        rows = pl.ds(pl.multiple_of(q * 256, 256), 256)
        part = jnp.dot(gt[do, rows], hidc[do], preferred_element_type=F32)
        gw_ref[rows, :] = (acc[rows, :] + part).astype(BF)
        return 0

    lax.fori_loop(0, 4, far, 0)
    phase(2)

    h_drain()
    t_drain()
    for copy in x_sends + x_relays + x_fwd + g_own + [swap]:
        copy.wait_send()
    for i in range(2):
        for way in range(2):
            g_relay(way, i).wait_send()
    for k in range(1, 16):
        p = lax.rem(me + k, 16)
        remote(st0, st1.at[me], s1s.at[k], s1r.at[me], dev(y, p // 2, lax.rem(p, 2))).wait_send()
    for k in range(1, NY):
        p = lax.rem(y + k, NY)
        remote(st2s, st2.at[y], s2s.at[k], s2r.at[y], dev(p, z, c)).wait_send()


def shards(hidden, weight, teacher, block_ids):
    first = lax.axis_index("vocab") * (V // BLK)
    owned = first + jnp.arange(V // BLK, dtype=jnp.int32)
    slots = jnp.arange(block_ids.shape[1], dtype=jnp.int32)
    sel = jnp.max(jnp.where(block_ids[:, None, :] == owned[None, :, None], slots, -1), axis=2)
    vm = pltpu.VMEM
    dma = pltpu.SemaphoreType.DMA
    return pl.pallas_call(
        kernel,
        out_shape=(jax.ShapeDtypeStruct((4, D), BF), jax.ShapeDtypeStruct((V, DC), BF)),
        in_specs=[pl.BlockSpec(memory_space=pl.ANY)] * 3
        + [pl.BlockSpec(memory_space=pltpu.SMEM)],
        out_specs=(pl.BlockSpec(memory_space=vm), pl.BlockSpec(memory_space=vm)),
        scratch_shapes=[
            vm((V, D), BF),
            vm((NY, NZ, 2, 4, D), BF),
            vm((T, D), BF),
            vm((NY, NZ, 2, 2, BLK, BLK), BF),
            vm((NX, NY, NZ, 2, 4, DC), BF),
            vm((NX, T, DC), BF),
            vm((2, 2, NZ, 4, DC), BF),
            vm((V, T), F32),
            vm((NX, V, T), BF),
            vm((T, V), BF),
            vm((NY, NZ, 2, 4, D), BF),
            vm((NY, NZ, 4, D), BF),
            vm((NY, NZ, 4, D), BF),
            vm((32, 4, D), BF),
            vm((8, 4, D), BF),
            vm((8, 4, D), F32),
            vm((8, 4, D), BF),
            vm((4, T), F32),
            vm((16, 4, T), F32),
            vm((4, T), F32),
            vm((NY, 4, T), F32),
            vm((V, DC), F32),
            dma((3,)),
            dma((2, 2, 4)), dma((2, 2, 4)), dma((8,)), dma((8,)),
            dma((2, 2, 4)), dma((2, 2, 4)), dma((8,)), dma((8,)),
            dma((6,)), dma((6,)), dma((3,)), dma((3,)),
            dma((16,)), dma((16,)), dma((4,)), dma((4,)),
            dma((2, 6)), dma((2, 6)), dma((1,)), dma((1,)),
            dma((8,)), dma((8,)), dma((8,)), dma((8,)),
        ],
        compiler_params=pltpu.CompilerParams(
            collective_id=0, has_side_effects=True, vmem_limit_bytes=60 << 20),
    )(hidden, weight, teacher.reshape(2, BLK, BLK), sel.reshape(-1))


def solution(mesh):
    placed = (P(("dp", "vocab"), None), P("vocab", None), P("dp", "vocab"), P("dp", None))
    return jax.shard_map(
        shards,
        mesh=mesh,
        in_specs=placed,
        out_specs=(P(("dp", "vocab"), None), P("vocab", "dp")),
        check_vma=False,
    )
```

```python
import jax
import jax.numpy as jnp
from jax import lax
from jax.experimental import pallas as pl
from jax.experimental.pallas import tpu as pltpu
from jax.sharding import PartitionSpec as P

BLK = 128
loss_scale = 1024.0
BF = jnp.bfloat16
F32 = jnp.float32
MESH = pl.DeviceIdType.MESH

D = 4096
V = 1024
T = 256
DC = 1024
NX, NY, NZ = 4, 4, 8


def kernel(hidden_ref, weight_ref, teacher_ref, ids_ref, gh_ref, gw_ref,
           w, hraw, hid, tea, craw, hidc, rel, logits, gt, g, graw, pair, ssum, r1, s2, s2f, r2,
           st0, st1, st2s, st2, acc, sel_ref,
           loc_sem, hs, hr, hs2, hr2, hfs, hfr, ts, tr, ts2, tr2, tfs, tfr, xs, xr, xfs, xfr,
           s1s, s1r, s2s, s2r, gs, gr, ps, pr, r1s, r1r, r2s, r2r):
    d = lax.axis_index("dp")
    v = lax.axis_index("vocab")
    y = v // (2 * NZ)
    z = lax.rem(v // 2, NZ)
    c = lax.rem(v, 2)
    me = lax.rem(v, 2 * NZ)

    def dev(yy, zz, cc):
        return {"dp": d, "vocab": (yy * NZ + zz) * 2 + cc}

    def xdev(dd):
        return {"dp": dd, "vocab": v}

    sib = dev(y, z, 1 - c)
    dr, dl, do = lax.rem(d + 1, NX), lax.rem(d + 3, NX), lax.rem(d + 2, NX)

    def remote(src, dst, s, r, device):
        return pltpu.make_async_remote_copy(src_ref=src, dst_ref=dst, send_sem=s, recv_sem=r,
                                            device_id=device, device_id_type=MESH)

    copy_h = pltpu.make_async_copy(hidden_ref, hraw.at[y, z, c], loc_sem.at[0])
    copy_t = pltpu.make_async_copy(teacher_ref, tea.at[y, z, c], loc_sem.at[1])
    copy_w = pltpu.make_async_copy(weight_ref, w, loc_sem.at[2])
    copy_h.start()
    copy_t.start()
    copy_w.start()

    barrier = pltpu.get_barrier_semaphore()
    for k in range(1, 16):
        p = lax.rem(me + k, 16)
        pl.semaphore_signal(barrier, inc=1, device_id=dev(y, p // 2, lax.rem(p, 2)),
                            device_id_type=MESH)
    for k in range(1, NY):
        pl.semaphore_signal(barrier, inc=1, device_id=dev(lax.rem(y + k, NY), z, c),
                            device_id_type=MESH)
    for dd in (dr, dl):
        pl.semaphore_signal(barrier, inc=1, device_id=xdev(dd), device_id_type=MESH)
    def find(k, slots):
        out = []
        for tb in range(2):
            entry = ids_ref[tb, k] - v * (V // BLK)
            for j in range(V // BLK):
                out.append(jnp.where(entry == j, k, slots[tb * 8 + j]))
        return tuple(out)

    for i, slot in enumerate(lax.fori_loop(0, 64, find, (jnp.int32(-1),) * 16)):
        sel_ref[i] = slot
    pl.semaphore_wait(barrier, 20)

    def gather(buf, half, ss1, sr1, ss2, sr2, fss, frs):
        def build(cc):
            if cc == 0:
                n1, p1, n2, p2 = NY, y, NZ, z
                at = lambda a, b: buf.at[a, b, cc]
                dev1, dev2 = (lambda a: dev(a, z, cc)), (lambda b: dev(y, b, cc))
            else:
                n1, p1, n2, p2 = NZ, z, NY, y
                at = lambda a, b: buf.at[b, a, cc]
                dev1, dev2 = (lambda a: dev(y, a, cc)), (lambda b: dev(b, z, cc))
            h1, h2 = n1 // 2, n2 // 2

            def one(way, s, come):
                sign = 1 - 2 * way
                ref = at(lax.rem(p1 - sign * (s - 1 + come) + n1, n1), p2)
                if s == h1:
                    ref = half(ref, way)
                return remote(ref, ref, ss1.at[way, s - 1], sr1.at[way, s - 1],
                              dev1(lax.rem(p1 + sign + n1, n1)))

            def two(j, way, s, come):
                sign = 1 - 2 * way
                ref = at(lax.rem(p1 + j + n1, n1), lax.rem(p2 - sign * (s - 1 + come) + n2, n2))
                if s == h2:
                    ref = half(ref, way)
                i = ((j % n1) * 2 + way) * h2 + s - 1
                return remote(ref, ref, ss2.at[i], sr2.at[i], dev2(lax.rem(p2 + sign + n2, n2)))

            offsets = [0] + [sign * k for k in range(1, h1) for sign in (-1, 1)] + [h1]

            def spread(j):
                for way in range(2):
                    two(j, way, 1, 0).start()

            def wave(w):
                if w == 0:
                    for way in range(2):
                        one(way, 1, 0).start()
                    spread(0)
                elif w <= h1:
                    for way in range(2):
                        one(way, w, 1).wait_recv()
                        if w < h1:
                            one(way, w + 1, 0).start()
                            spread(-w if way == 0 else w)
                    if w == h1:
                        spread(h1)
                for j in reversed(offsets):
                    s = w - abs(j)
                    if 1 <= s <= h2:
                        for way in range(2):
                            two(j, way, s, 1).wait_recv()
                            if s < h2:
                                two(j, way, s + 1, 0).start()

            def drain():
                for way in range(2):
                    for s in range(1, h1 + 1):
                        one(way, s, 0).wait_send()
                    for j in offsets:
                        for s in range(1, h2 + 1):
                            two(j, way, s, 0).wait_send()

            return wave, drain

        (wave_a, drain_a), (wave_b, drain_b) = build(0), build(1)

        def forward(k, cc):
            unit = buf.at[:, lax.rem(z + k, NZ), cc]
            return remote(unit, unit, fss.at[k], frs.at[k], sib)

        def wave(w):
            pl.when(c == 0)(lambda: wave_a(w))
            pl.when(c == 1)(lambda: wave_b(w))
            if w >= 2:
                for k in sorted({w - 2, (NZ - w + 2) % NZ}):
                    forward(k, c).start()

        def drain():
            pl.when(c == 0)(drain_a)
            pl.when(c == 1)(drain_b)
            for k in range(NZ):
                forward(k, c).wait_send()

        def from_sibling():
            for k in range(NZ):
                forward(k, 1 - c).wait_recv()

        return wave, drain, from_sibling

    h_wave, h_drain, h_sib = gather(
        hraw, lambda ref, way: ref.at[:, pl.ds(way * (D // 2), D // 2)],
        hs, hr, hs2, hr2, hfs, hfr)
    t_wave, t_drain, t_sib = gather(
        tea, lambda ref, way: ref.at[way], ts, tr, ts2, tr2, tfs, tfr)
    copy_h.wait()
    copy_t.wait()
    for i in range(7):
        h_wave(i)
        if 3 <= i < 6:
            t_wave(i - 3)
    def cols(dd):
        return pl.ds(pl.multiple_of(dd * DC, DC), DC)

    x_sends = [
        remote(hraw.at[0:2, :, c, :, cols(do)], rel.at[0], xs.at[0], xr.at[0], xdev(dr)),
        remote(hraw.at[2:4, :, c, :, cols(do)], rel.at[1], xs.at[1], xr.at[1], xdev(dl)),
        remote(hraw.at[:, :, c, :, cols(dr)], craw.at[d, :, :, c], xs.at[2], xr.at[2], xdev(dr)),
        remote(hraw.at[:, :, c, :, cols(dl)], craw.at[d, :, :, c], xs.at[3], xr.at[3], xdev(dl)),
    ]
    for copy in x_sends:
        copy.start()
    x_relays = [
        remote(rel.at[0], craw.at[dl, 0:2, :, c], xs.at[4], xr.at[4], xdev(dr)),
        remote(rel.at[1], craw.at[dr, 2:4, :, c], xs.at[5], xr.at[5], xdev(dl)),
    ]
    t_wave(3)
    h_sib()

    def flatten(i, _):
        yy, zz = i // 4, lax.rem(i, 4)
        hid[pl.ds(pl.multiple_of(16 * i, 16), 16), :] = hraw[yy, pl.ds(2 * zz, 2)].reshape(16, D)
        return 0

    lax.fori_loop(0, 16, flatten, 0)
    copy_w.wait()
    top = jnp.full((1, T), -jnp.inf, F32)
    for q in range(4):
        rows = pl.ds(256 * q, 256)
        part = lax.dot_general(w[rows, :], hid[...], (((1,), (1,)), ((), ())),
                               preferred_element_type=F32)
        logits[rows, :] = part
        top = jnp.maximum(top, jnp.max(part, axis=0, keepdims=True))
        if q == 0:
            t_wave(4)
        if q == 2:
            t_wave(5)
    total = jnp.zeros((1, T), F32)
    for q in range(4):
        rows = pl.ds(256 * q, 256)
        total = total + jnp.sum(jnp.exp(logits[rows, :] - top), axis=0, keepdims=True)
    mass = lax.dot_general(jnp.ones((8, BLK), BF), tea[y, z, c].reshape(T, BLK),
                           (((1,), (1,)), ((), ())), preferred_element_type=F32)[0:1]
    st0[0:1, :] = top
    st0[1:2, :] = total
    st0[2:3, :] = mass
    st0[3:4, :] = mass
    for k in range(1, 16):
        p = lax.rem(me + k, 16)
        remote(st0, st1.at[me], s1s.at[k], s1r.at[me], dev(y, p // 2, lax.rem(p, 2))).start()
    t_wave(6)
    for k in range(1, 16):
        p = lax.rem(me + k, 16)
        remote(st0, st1.at[p], s1s.at[k], s1r.at[p], dev(y, p // 2, lax.rem(p, 2))).wait_recv()

    def merge(parts):
        m = parts[0][0:1]
        for part in parts[1:]:
            m = jnp.maximum(m, part[0:1])
        s = jnp.zeros((1, T), F32)
        a = jnp.zeros((1, T), F32)
        for part in parts:
            s = s + part[1:2] * jnp.exp(part[0:1] - m)
            a = a + part[2:3]
        return m, s, a

    m1, s1, a1 = merge([st0[...]] + [st1[lax.rem(me + k, 16)] for k in range(1, 16)])
    st2s[0:1, :] = m1
    st2s[1:2, :] = s1
    st2s[2:3, :] = a1
    st2s[3:4, :] = a1
    for k in range(1, NY):
        p = lax.rem(y + k, NY)
        remote(st2s, st2.at[y], s2s.at[k], s2r.at[y], dev(p, z, c)).start()
    x_sends[0].wait_recv()
    x_relays[0].start()
    x_sends[1].wait_recv()
    x_relays[1].start()
    for k in range(1, NY):
        p = lax.rem(y + k, NY)
        remote(st2s, st2.at[p], s2s.at[k], s2r.at[p], dev(p, z, c)).wait_recv()
    m2, s2_, a2 = merge([st2s[...]] + [st2[lax.rem(y + k, NY)] for k in range(1, NY)])
    scale = loss_scale * a2 / s2_
    t_sib()

    def grads(j, _):
        rows = pl.ds(pl.multiple_of(j * BLK, BLK), BLK)
        for tb in range(2):
            k = sel_ref[tb * 8 + j]
            found = jnp.where(k >= 0, loss_scale, 0.0)
            kk = jnp.maximum(k, 0)
            tile = tea[kk // 16, lax.rem(kk // 2, NZ), lax.rem(kk, 2), tb]
            part = slice(tb * BLK, tb * BLK + BLK)
            value = (scale[:, part] * jnp.exp(logits[rows, part] - m2[:, part])
                     - found * tile.astype(F32).T)
            gt[d, rows, part] = value.astype(BF)
        return 0

    lax.fori_loop(0, 8, grads, 0)

    def chunk(dd, q):
        return gt.at[dd, pl.ds(256 * q, 256)]
    g_own = []
    for i in range(4):
        for way, q, to in ((0, i, dr), (1, (i + 2) % 4, dl)):
            copy = remote(chunk(d, q), chunk(d, q), gs.at[way, i], gr.at[way, i], xdev(to))
            copy.start()
            g_own.append(copy)

    def g_arrived(way, i):
        q, origin = ((i, dl), ((i + 2) % 4, dr))[way]
        to = (dr, dl)[way]
        remote(chunk(origin, q), chunk(origin, q), gs.at[way, i], gr.at[way, i],
               xdev(to)).wait_recv()

    def g_relay(way, i):
        q, origin = ((i, dl), ((i + 2) % 4, dr))[way]
        to = (dr, dl)[way]
        return remote(chunk(origin, q), chunk(origin, q), gs.at[way, 4 + i], gr.at[way, 4 + i],
                      xdev(to))
    g[...] = gt[d].T
    H = D // 2

    def part_of(half):
        return pl.ds(half * H, H)

    swap = [remote(graw.at[:, :, 1 - c, :, part_of(half)], pair.at[:, :, :, part_of(half)],
                   ps.at[half], pr.at[half], sib) for half in range(2)]

    for half in range(2):
        def back(i, _):
            span = pl.ds(pl.multiple_of(i * 512, 512), 512)
            value = jnp.dot(g[...], w[:, span], preferred_element_type=F32)
            graw[:, :, :, :, span] = value.reshape(NY, NZ, 2, 4, 512).astype(BF)
            return 0

        lax.fori_loop(half * 4, half * 4 + 4, back, 0)
        swap[half].start()

    def reducer(half, z_first):
        span = part_of(half)
        if z_first:
            n1, p1, n2, p2 = NZ, z, NY, y
            piece = lambda o: ssum.at[:, o, :, span]
            own = lambda o: (graw[o, z, c, :, span].astype(F32) + pair[o, z, :, span].astype(F32))
            dev1, dev2 = (lambda o: dev(y, o, c)), (lambda o: dev(o, z, c))
        else:
            n1, p1, n2, p2 = NY, y, NZ, z
            piece = lambda o: ssum.at[o, :, :, span]
            own = lambda o: (graw[y, o, c, :, span].astype(F32) + pair[y, o, :, span].astype(F32))
            dev1, dev2 = (lambda o: dev(o, z, c)), (lambda o: dev(y, o, c))

        def one(k, come):
            o = lax.rem(p1 + k, n1)
            to = o if come else p1
            return remote(piece(o), r1.at[pl.ds(to * n2, n2), :, span], r1s.at[half, k],
                          r1r.at[half, to], dev1(o))

        def two(k, come):
            o = lax.rem(p2 + k, n2)
            to = o if come else p2
            return remote(s2.at[o, :, span], r2.at[to, :, span], r2s.at[half, k],
                          r2r.at[half, to], dev2(o))

        def start():
            for k in range(1, n1):
                one(k, False).start()

        def middle():
            for k in range(1, n1):
                one(k, True).wait_recv()

            def add(i, _):
                value = own(i)
                for k in range(1, n1):
                    value = value + r1[lax.rem(p1 + k, n1) * n2 + i, :, span].astype(F32)
                s2f[i, :, span] = value
                s2[i, :, span] = value.astype(BF)
                return 0

            lax.fori_loop(0, n2, add, 0)
            for k in range(1, n2):
                two(k, False).start()

        def finish():
            for k in range(1, n2):
                two(k, True).wait_recv()
            value = s2f[p2, :, span]
            for k in range(1, n2):
                value = value + r2[lax.rem(p2 + k, n2), :, span].astype(F32)
            gh_ref[:, span] = value.astype(BF)
            for k in range(1, n1):
                one(k, False).wait_send()
            for k in range(1, n2):
                two(k, False).wait_send()

        return start, middle, finish

    reduce_z, reduce_y = reducer(0, True), reducer(0, False)
    reduce_1 = reducer(1, False)

    def phase(half, i):
        if half == 0:
            pl.when(c == 0)(reduce_z[i])
            pl.when(c == 1)(reduce_y[i])
        else:
            reduce_1[i]()

    for half in range(2):
        swap[half].wait_recv()
        span = part_of(half)

        def add_pair(i, _):
            yy, zz = i // NZ, lax.rem(i, NZ)
            ssum[yy, zz, :, span] = (graw[yy, zz, c, :, span].astype(F32)
                                     + pair[yy, zz, :, span].astype(F32)).astype(BF)
            return 0
        lax.fori_loop(0, 32, add_pair, 0)
        phase(half, 0)
    for i in range(2):
        for way in range(2):
            g_arrived(way, i)
            g_relay(way, i).start()
    x_sends[2].wait_recv()
    x_sends[3].wait_recv()
    x_relays[0].wait_recv()
    x_relays[1].wait_recv()
    x_fwd = [remote(craw.at[dd, :, :, c], craw.at[dd, :, :, c], xfs.at[i], xfr.at[i], sib)
             for i, dd in enumerate((dl, dr, do))]
    for copy in x_fwd:
        copy.start()
    for i, dd in enumerate((dl, dr, do)):
        remote(craw.at[dd, :, :, 1 - c], craw.at[dd, :, :, 1 - c], xfs.at[i], xfr.at[i],
               sib).wait_recv()
    for dd in (dl, dr, do):
        def flatten_cols(i, _, dd=dd):
            yy, zz = i // 4, lax.rem(i, 4)
            hidc[dd, pl.ds(pl.multiple_of(16 * i, 16), 16), :] = (
                craw[dd, yy, pl.ds(2 * zz, 2)].reshape(16, DC))
            return 0

        lax.fori_loop(0, 16, flatten_cols, 0)
    hidc[d] = hid[:, cols(d)]
    for i in range(2, 4):
        for way in range(2):
            g_arrived(way, i)

    def near(q, _):
        rows = pl.ds(pl.multiple_of(q * 256, 256), 256)
        part = jnp.dot(gt[d, rows], hidc[d], preferred_element_type=F32)
        part = part + jnp.dot(gt[dl, rows], hidc[dl], preferred_element_type=F32)
        part = part + jnp.dot(gt[dr, rows], hidc[dr], preferred_element_type=F32)
        acc[rows, :] = part
        return 0
    lax.fori_loop(0, 4, near, 0)
    phase(0, 1)
    phase(1, 1)

    for i in range(2):
        for way, q in ((0, i), (1, (i + 2) % 4)):
            remote(chunk(do, q), chunk(do, q), gs.at[way, 4 + i], gr.at[way, 4 + i],
                   xdev((dr, dl)[way])).wait_recv()
            rows = pl.ds(q * 256, 256)
            value = jnp.dot(gt[do, rows], hidc[do], preferred_element_type=F32)
            gw_ref[rows, :] = (acc[rows, :] + value).astype(BF)
    phase(0, 2)
    phase(1, 2)
    h_drain()
    t_drain()
    for copy in x_sends + x_relays + x_fwd + g_own + swap:
        copy.wait_send()
    for i in range(2):
        for way in range(2):
            g_relay(way, i).wait_send()
    for k in range(1, 16):
        p = lax.rem(me + k, 16)
        remote(st0, st1.at[me], s1s.at[k], s1r.at[me], dev(y, p // 2, lax.rem(p, 2))).wait_send()
    for k in range(1, NY):
        p = lax.rem(y + k, NY)
        remote(st2s, st2.at[y], s2s.at[k], s2r.at[y], dev(p, z, c)).wait_send()


def shards(hidden, weight, teacher, block_ids):
    vm = pltpu.VMEM
    dma = pltpu.SemaphoreType.DMA
    return pl.pallas_call(
        kernel,
        out_shape=(jax.ShapeDtypeStruct((4, D), BF), jax.ShapeDtypeStruct((V, DC), BF)),
        in_specs=[pl.BlockSpec(memory_space=pl.ANY)] * 3
        + [pl.BlockSpec(memory_space=pltpu.SMEM)],
        out_specs=(pl.BlockSpec(memory_space=vm), pl.BlockSpec(memory_space=vm)),
        scratch_shapes=[
            vm((V, D), BF),
            vm((NY, NZ, 2, 4, D), BF),
            vm((T, D), BF),
            vm((NY, NZ, 2, 2, BLK, BLK), BF),
            vm((NX, NY, NZ, 2, 4, DC), BF),
            vm((NX, T, DC), BF),
            vm((2, 2, NZ, 4, DC), BF),
            vm((V, T), F32),
            vm((NX, V, T), BF),
            vm((T, V), BF),
            vm((NY, NZ, 2, 4, D), BF),
            vm((NY, NZ, 4, D), BF),
            vm((NY, NZ, 4, D), BF),
            vm((32, 4, D), BF),
            vm((8, 4, D), BF),
            vm((8, 4, D), F32),
            vm((8, 4, D), BF),
            vm((4, T), F32),
            vm((16, 4, T), F32),
            vm((4, T), F32),
            vm((NY, 4, T), F32),
            vm((V, DC), F32),
            pltpu.SMEM((16,), jnp.int32),
            dma((3,)),
            dma((2, 4)), dma((2, 4)), dma((32,)), dma((32,)), dma((8,)), dma((8,)),
            dma((2, 4)), dma((2, 4)), dma((32,)), dma((32,)), dma((8,)), dma((8,)),
            dma((6,)), dma((6,)), dma((3,)), dma((3,)),
            dma((16,)), dma((16,)), dma((4,)), dma((4,)),
            dma((2, 6)), dma((2, 6)), dma((2,)), dma((2,)),
            dma((2, 8)), dma((2, 8)), dma((2, 8)), dma((2, 8)),
        ],
        compiler_params=pltpu.CompilerParams(
            collective_id=0, has_side_effects=True, vmem_limit_bytes=60 << 20),
    )(hidden, weight, teacher.reshape(2, BLK, BLK), block_ids)


def solution(mesh):
    placed = (P(("dp", "vocab"), None), P("vocab", None), P("dp", "vocab"), P("dp", None))
    return jax.shard_map(
        shards,
        mesh=mesh,
        in_specs=placed,
        out_specs=(P(("dp", "vocab"), None), P("vocab", "dp")),
        check_vma=False,
    )
```
